128 devices in a mesh: row: 8 (over x, z_lo), col: 16 (over y, z_hi, core).
Axes of the slice: x: 4, y: 4, z: 4 (z_hi: 2, z_lo: 2; z = z_hi * 2 + z_lo), core: 2. Of those that a mesh axis runs over, the one named last changes fastest.
Arguments:
- momentum: bfloat16 [16384, 16384], P('row', 'col'), may hold values from -6 to 6
- gradient: bfloat16 [16384, 16384], P('row', 'col'), may hold values from -43 to 43
- right_prev: float32 [16384, 512], P('col'), may hold values from -6 to 6
- weight: bfloat16 [16384, 16384], P('col', 'row'), may hold values from -0.046875 to 0.046875
- tokens: bfloat16 [256, 16384], P(None, 'row'), may hold values from -6 to 6
Outputs:
- new_momentum: bfloat16 [16384, 16384], P('row', 'col')
- new_basis: float32 [16384, 512], P('col')
- new_weight: bfloat16 [16384, 16384], P('col', 'row')
- projected: bfloat16 [256, 16384], P('row', 'col')
The draws below stay inside these ranges and needn't reach their ends.
All inputs are finite; a program needn't handle non-finite values.
Results may differ from the reference program's by a relative error of at most 0.006.
Values may be sent and summed in bfloat16 or wider, within the bound.
No kernel may reach another device: no remote copies, remote signals or barrier semaphores. Data moves between devices by JAX's collectives and lax.ppermute only.
A program may use at most 128 MiB of HBM per device.

```python
import math
import jax
import jax.numpy as jnp
from jax import lax

DOUT = 16384
DIN = 16384
RANK = 512
TOK = 256


def draw_gradient(key, part):
    factor_rank = max(RANK // 4, 1)
    left_key = jax.random.fold_in(key, 11)
    right_key = jax.random.fold_in(key, 12)
    noise_key = jax.random.fold_in(key, 13)
    left_part = jnp.clip(jax.random.normal(left_key, (DOUT, factor_rank), jnp.float32), -5.0, 5.0)
    right_part = jnp.clip(jax.random.normal(right_key, (DIN, factor_rank), jnp.float32), -5.0, 5.0)
    shared = jnp.dot(left_part, right_part.T, precision=lax.Precision.HIGHEST, preferred_element_type=jnp.float32) / math.sqrt(factor_rank)
    position = jnp.arange(DIN, dtype=jnp.float32).reshape(1, DIN) / max(DIN - 1, 1)
    rising = 1.0 + 3.0 * position
    noise = 0.5 * jnp.clip(jax.random.normal(noise_key, (DOUT, DIN), jnp.float32), -6.0, 6.0)
    values = 3.35 * shared * rising + noise
    return jnp.clip(values, -43.0, 43.0).astype(jnp.bfloat16)


def levels(key, extent, cuts, low, top_value):
    def one(axis_at, parts):
        steps = jax.random.uniform(jax.random.fold_in(jax.random.fold_in(key, 6), axis_at), (parts,), jnp.float32, low / len(cuts), top_value / len(cuts))
        return jnp.repeat(jnp.exp(steps), extent[axis_at] // parts).reshape((-1,) + (1,) * (len(extent) - axis_at - 1))

    loudness = one(*cuts[0])
    for cut in cuts[1:]:
        loudness = loudness * one(*cut)
    return loudness


def normal_values(stream_key, dims, deviation, reach, shards=(), held_as=jnp.bfloat16):
    array = jax.random.normal(stream_key, dims, jnp.float32) * deviation
    if len(shards) > 0:
        array = levels(stream_key, dims, shards, -0.22, 0.18) * array
    return jnp.clip(array, min=-reach, max=reach).astype(held_as)


def setup_inputs(seed: int = 0) -> dict:
    key_list = jax.random.split(jax.random.key(seed), 6)
    return {
        "momentum": normal_values(key_list[0], (DOUT, DIN), 1.0, 6.0, ((0, 8), (1, 16))),
        "gradient": draw_gradient(jax.random.fold_in(key_list[5], 71), 0),
        "right_prev": normal_values(key_list[2], (DIN, RANK), 1.0, 6.0, ((0, 16),), jnp.float32),
        "weight": normal_values(key_list[3], (DOUT, DIN), DIN ** -0.5, 0.046875, ((0, 16), (1, 8))),
        "tokens": normal_values(key_list[4], (TOK, DIN), 1.0, 6.0, ((1, 8),)),
    }


decay_part = 0.05
step_size = 0.01
epsilon = 1e-06

def reference(momentum, gradient, right_prev, weight, tokens):
    highest = lax.Precision.HIGHEST
    mixed = momentum.astype(jnp.float32) + gradient.astype(jnp.float32)
    left_raw = jnp.dot(mixed.astype(jnp.float32), right_prev.astype(jnp.float32), precision=highest, preferred_element_type=jnp.float32)
    gram_matrix = jnp.dot(left_raw.T.astype(jnp.float32), left_raw.astype(jnp.float32), precision=highest, preferred_element_type=jnp.float32)
    factor = jnp.linalg.cholesky(gram_matrix)
    left_factor = lax.linalg.triangular_solve(factor, left_raw, left_side=False, lower=True, transpose_a=True)
    right_factor = jnp.dot(mixed.T.astype(jnp.float32), left_factor.astype(jnp.float32), precision=highest, preferred_element_type=jnp.float32)
    outer = jnp.dot(left_factor.astype(jnp.float32), right_factor.T.astype(jnp.float32), precision=highest, preferred_element_type=jnp.float32)
    new_momentum = (mixed - decay_part * outer).astype(jnp.bfloat16)
    squares = lax.optimization_barrier(jnp.sum(right_factor * right_factor, axis=0))
    new_basis = right_factor * lax.rsqrt(squares / DIN + epsilon)
    left_send = left_factor.astype(jnp.bfloat16)
    basis_send = new_basis.astype(jnp.bfloat16)
    update = jnp.dot(left_send.astype(jnp.float32), basis_send.T.astype(jnp.float32), preferred_element_type=jnp.float32)
    new_weight = (weight.astype(jnp.float32) - step_size * update).astype(jnp.bfloat16)
    projected = jnp.dot(tokens.astype(jnp.float32), new_weight.T.astype(jnp.float32), preferred_element_type=jnp.float32).astype(jnp.bfloat16)
    return (new_momentum, new_basis, new_weight, projected)
```

```python
import jax
import jax.numpy as jnp
from jax import lax
from jax.sharding import Mesh
from jax.sharding import PartitionSpec as P

DIN = 16384
COL = ("col_0", "col_1", "col_2")
ROW = ("row_0", "row_1")
ALL = ROW + COL
CORE = "col_2"
CHIPS = ("col_0", "col_1")

decay_part = 0.05
step_size = 0.01
epsilon = 1e-06

HIGH = lax.Precision.HIGH
HIGHEST = lax.Precision.HIGHEST


def dot(lhs, rhs, dims, precision=None):
    return lax.dot_general(
        lhs, rhs, ((dims[:1], dims[1:]), ((), ())), precision=precision, preferred_element_type=jnp.float32
    )


def scatter_sum(array, axes, length):
    pieces = array.reshape(length, array.shape[0] // length, *array.shape[1:])
    return jnp.sum(lax.all_to_all(pieces, axes, 0, 0, tiled=True).astype(jnp.float32), axis=0)


def gathered(array, axes, length):
    pieces = lax.all_to_all(
        jnp.broadcast_to(array[None], (length, *array.shape)), axes, 0, 0, tiled=True
    )
    return pieces.reshape(length * array.shape[0], *array.shape[1:])


def to_other_core(array):
    return lax.ppermute(array, CORE, [(0, 1), (1, 0)])


def both_halves(own, core):
    other = to_other_core(own)
    return jnp.where(
        core == 0, jnp.concatenate([own, other], axis=0), jnp.concatenate([other, own], axis=0)
    )


def to_tile_owner(array):
    pairs = [(r * 16 + 2 * j + k, j * 16 + 2 * r + k) for r in range(8) for j in range(8) for k in range(2)]
    return lax.ppermute(array, ALL, pairs)


def per_device(momentum, gradient, right_prev, weight, tokens):
    core = lax.axis_index(CORE)
    mixed = momentum.astype(jnp.float32) + gradient.astype(jnp.float32)
    partial_left = dot(mixed, right_prev, (1, 0), HIGH)
    halves = partial_left.reshape(2, 1024, 512)
    sent = lax.dynamic_index_in_dim(halves, 1 - core, 0, keepdims=False)
    kept = lax.dynamic_index_in_dim(halves, core, 0, keepdims=False)
    left_shard = scatter_sum(kept + to_other_core(sent), CHIPS, 8)

    gram_partial = dot(left_shard, left_shard, (0, 0), HIGHEST)
    gram_matrix = gathered(scatter_sum(gram_partial, ALL, 128), ALL, 128)
    factor = jnp.linalg.cholesky(gram_matrix)
    inverse = lax.linalg.triangular_solve(
        factor, jnp.eye(512, dtype=jnp.float32), left_side=True, lower=True
    )

    left_rows = both_halves(gathered(left_shard, CHIPS, 8), core)
    partial_right = dot(mixed, left_rows, (0, 0), HIGH)
    right_shard = scatter_sum(partial_right, ROW, 8)
    tile_left_raw = gathered(to_tile_owner(left_shard), ROW, 8)
    tile_right_raw = to_tile_owner(right_shard)

    right_own = dot(right_shard, inverse, (1, 1), HIGHEST)
    squares = jnp.sum(gathered(jnp.sum(right_own * right_own, axis=0)[None], ALL, 128), axis=0)
    scale = lax.rsqrt(squares / DIN + epsilon)
    right_factor = gathered(right_own.astype(jnp.bfloat16), ROW, 8)
    new_basis = right_factor.astype(jnp.float32) * scale
    left_factor = dot(left_rows, inverse, (1, 1), HIGH).astype(jnp.bfloat16)
    outer = dot(left_factor, right_factor, (1, 1))
    new_momentum = (mixed - decay_part * outer).astype(jnp.bfloat16)

    tile_right = dot(tile_right_raw, inverse, (1, 1), HIGHEST).astype(jnp.bfloat16)
    tile_right = both_halves(gathered(tile_right, CHIPS, 8), core)
    tile_left = (dot(tile_left_raw, inverse, (1, 1), HIGH) * scale).astype(jnp.bfloat16)
    update = dot(tile_left, tile_right, (1, 1))
    new_weight = (weight.astype(jnp.float32) - step_size * update).astype(jnp.bfloat16)
    partial_projected = dot(tokens, new_weight, (1, 1)).astype(jnp.bfloat16)
    projected = scatter_sum(partial_projected, ROW, 8).astype(jnp.bfloat16)
    return (new_momentum, new_basis, new_weight, projected)


def solution(mesh):
    torus = Mesh(mesh.devices.reshape(4, 2, 4, 2, 2), ("row_0", "row_1", "col_0", "col_1", "col_2"))
    placed = (P(ROW, COL), P(ROW, COL), P(COL, None), P(COL, ROW), P(None, ROW))
    return jax.shard_map(
        per_device,
        mesh=torus,
        in_specs=placed,
        out_specs=(P(ROW, COL), P(COL, None), P(COL, ROW), P(ROW, COL)),
        check_vma=False,
    )
```

```python
import jax
import jax.numpy as jnp
from jax import lax
from jax.experimental import pallas as pl
from jax.experimental.pallas import tpu as pltpu
from jax.sharding import Mesh
from jax.sharding import PartitionSpec as P

DIN = 16384
COL = ("col_0", "col_1", "col_2")
ROW = ("row_0", "row_1")
ALL = ROW + COL
CORE = "col_2"
CHIPS = ("col_0", "col_1")

decay_part = 0.05
step_size = 0.01
epsilon = 1e-06

HIGH = lax.Precision.HIGH
HIGHEST = lax.Precision.HIGHEST


def whole(v):
    return jnp.broadcast_to(v, (8, 128))


def eliminate(z_ref, u_ref):
    lane = lax.broadcasted_iota(jnp.int32, (8, 128), 1)
    sub = lax.broadcasted_iota(jnp.int32, (8, 128), 0)
    rows = [[z_ref[t, 8 * q:8 * q + 8, :] for t in range(4)] for q in range(16)]
    for p in range(16):
        columns = {}
        for q in range(p, 16):
            for i in range(8):
                columns[q, i] = whole(rows[q][0][:, 8 * p + i:8 * p + i + 1])
        pivot = {(i, j): whole(columns[p, j][i:i + 1, :]) for j in range(8) for i in range(j, 8)}
        own = (lane >= 8 * p) & (lane < 8 * p + 8)
        start = [jnp.where(own, jnp.where(sub == lane - 8 * p, 1.0, 0.0), rows[p][0])] + rows[p][1:]
        inv = {}
        low = {}
        for j in range(8):
            r = lax.rsqrt(pivot[j, j])
            col = {i: pivot[i, j] * r for i in range(j + 1, 8)}
            for k in range(j + 1, 8):
                for i in range(k, 8):
                    pivot[i, k] = pivot[i, k] - col[i] * col[k]
            for m in range(j):
                inv[j, m] = pivot[j, m, "sum"] * (-r)
            inv[j, j] = r
            for i in range(j + 1, 8):
                for m in range(j + 1):
                    term = col[i] * inv[j, m]
                    pivot[i, m, "sum"] = term if m == j else pivot[i, m, "sum"] + term
        first = [[whole(start[t][i:i + 1, :]) for i in range(8)] for t in range(4)]
        solved = []
        for t in range(4):
            lows = []
            for i in range(8):
                v = inv[i, 0] * first[t][0]
                for m in range(1, i + 1):
                    v = v + inv[i, m] * first[t][m]
                lows.append(v)
            out = lows[0]
            for i in range(1, 8):
                out = jnp.where(sub == i, lows[i], out)
            u_ref[t, 8 * p:8 * p + 8, :] = jnp.where(lane <= sub + 8 * p, out, 0.0) if t == 0 else out
            line = []
            for i in range(8):
                v = inv[7, i] * lows[7]
                for m in range(i, 7):
                    v = v + inv[m, i] * lows[m]
                line.append(v)
            solved.append(line)
        for q in range(p + 1, 16):
            for t in range(4):
                total = jnp.where(own, 0.0, rows[q][t]) if t == 0 else rows[q][t]
                for i in range(8):
                    total = total - columns[q, i] * solved[t][i]
                rows[q][t] = total

def factor_kernel(g_ref, x_ref, z_ref, d_ref, u_ref):
    z_ref[...] = g_ref[...]
    def step(k, carry):
        at = pl.multiple_of(k * 128, 128)
        places = [pl.multiple_of(lax.rem(k + t, 4) * 128, 128) for t in range(4)]
        for t in range(4):
            d_ref[t] = z_ref[pl.ds(at, 128), pl.ds(places[t], 128)]
        eliminate(d_ref, u_ref)
        for t in range(4):
            x_ref[pl.ds(at, 128), pl.ds(places[t], 128)] = jnp.where(places[t] <= at, u_ref[t], 0.0)
        for t in range(1, 4):
            @pl.when(places[t] > at)
            def _():
                lower = u_ref[t]
                rest = pl.ds(places[t], 128)
                for s in range(4):
                    change = lax.dot_general(lower, u_ref[s], (((0,), (0,)), ((), ())), precision=HIGHEST, preferred_element_type=jnp.float32)
                    if s == 0:
                        z_ref[rest, pl.ds(places[s], 128)] = -change
                    else:
                        z_ref[rest, pl.ds(places[s], 128)] -= change
        return carry
    lax.fori_loop(0, 4, step, 0)


def inverse_factor(gram):
    return pl.pallas_call(
        factor_kernel,
        out_shape=jax.ShapeDtypeStruct((512, 512), jnp.float32),
        scratch_shapes=[
            pltpu.VMEM((512, 512), jnp.float32),
            pltpu.VMEM((4, 128, 128), jnp.float32),
            pltpu.VMEM((4, 128, 128), jnp.float32),
        ],
        compiler_params=pltpu.CompilerParams(vmem_limit_bytes=16 * 1024 * 1024),
    )(gram)


def dot(lhs, rhs, dims, precision=None):
    return lax.dot_general(
        lhs, rhs, ((dims[:1], dims[1:]), ((), ())), precision=precision, preferred_element_type=jnp.float32
    )


def scatter_sum(array, axes, length):
    pieces = array.reshape(length, array.shape[0] // length, *array.shape[1:])
    return jnp.sum(lax.all_to_all(pieces, axes, 0, 0, tiled=True).astype(jnp.float32), axis=0)


def gathered(array, axes, length):
    pieces = lax.all_to_all(
        jnp.broadcast_to(array[None], (length, *array.shape)), axes, 0, 0, tiled=True
    )
    return pieces.reshape(length * array.shape[0], *array.shape[1:])


def gathered_by_permutes(array, axes, length):
    me = lax.axis_index(axes)
    rows = array.shape[0]
    joined = jnp.zeros((length * rows, *array.shape[1:]), array.dtype)
    joined = lax.dynamic_update_slice_in_dim(joined, array, me * rows, 0)
    for flip in range(1, length):
        piece = lax.ppermute(array, axes, [(i, i ^ flip) for i in range(length)])
        joined = lax.dynamic_update_slice_in_dim(joined, piece, (me ^ flip) * rows, 0)
    return joined


def to_other_core(array):
    return lax.ppermute(array, CORE, [(0, 1), (1, 0)])


def both_halves(own, core):
    other = to_other_core(own)
    return jnp.where(
        core == 0, jnp.concatenate([own, other], axis=0), jnp.concatenate([other, own], axis=0)
    )


def to_tile_owner(array):
    pairs = [(r * 16 + 2 * j + k, j * 16 + 2 * r + k) for r in range(8) for j in range(8) for k in range(2)]
    return lax.ppermute(array, ALL, pairs)


def per_device(momentum, gradient, right_prev, weight, tokens):
    core = lax.axis_index(CORE)
    mixed = momentum.astype(jnp.float32) + gradient.astype(jnp.float32)
    partial_left = dot(mixed, right_prev, (1, 0), HIGH)
    halves = partial_left.reshape(2, 1024, 512)
    sent = lax.dynamic_index_in_dim(halves, 1 - core, 0, keepdims=False)
    kept = lax.dynamic_index_in_dim(halves, core, 0, keepdims=False)
    left_shard = scatter_sum(kept + to_other_core(sent), CHIPS, 8)

    gram_partial = dot(left_shard, left_shard, (0, 0), HIGHEST)
    gram_matrix = gathered(scatter_sum(gram_partial, ALL, 128), ALL, 128)
    inverse = inverse_factor(gram_matrix)

    left_rows = both_halves(gathered_by_permutes(left_shard, CHIPS, 8), core)
    partial_right = dot(mixed, left_rows, (0, 0), HIGH)
    right_shard = scatter_sum(partial_right, ROW, 8)

    right_own = dot(right_shard, inverse, (1, 1), HIGHEST)
    right_send = right_own.astype(jnp.bfloat16)
    tile_right = both_halves(gathered_by_permutes(to_tile_owner(right_send), CHIPS, 8), core)
    squares = jnp.sum(gathered(jnp.sum(right_own * right_own, axis=0)[None], ALL, 128), axis=0)
    scale = lax.rsqrt(squares / DIN + epsilon)
    left_send = dot(to_tile_owner(left_shard), inverse, (1, 1), HIGH).astype(jnp.bfloat16)
    tile_left = gathered_by_permutes(left_send, ROW, 8)
    tile_left = (tile_left.astype(jnp.float32) * scale).astype(jnp.bfloat16)
    update = dot(tile_left, tile_right, (1, 1))
    new_weight = (weight.astype(jnp.float32) - step_size * update).astype(jnp.bfloat16)
    partial_projected = dot(tokens, new_weight, (1, 1)).astype(jnp.bfloat16)
    projected = scatter_sum(partial_projected, ROW, 8).astype(jnp.bfloat16)

    right_factor = gathered_by_permutes(right_send, ROW, 8)
    new_basis = right_factor.astype(jnp.float32) * scale
    left_factor = dot(left_rows, inverse, (1, 1), HIGH).astype(jnp.bfloat16)
    outer = dot(left_factor, right_factor, (1, 1))
    new_momentum = (mixed - decay_part * outer).astype(jnp.bfloat16)
    return (new_momentum, new_basis, new_weight, projected)


def solution(mesh):
    torus = Mesh(mesh.devices.reshape(4, 2, 4, 2, 2), ("row_0", "row_1", "col_0", "col_1", "col_2"))
    placed = (P(ROW, COL), P(ROW, COL), P(COL, None), P(COL, ROW), P(None, ROW))
    return jax.shard_map(
        per_device,
        mesh=torus,
        in_specs=placed,
        out_specs=(P(ROW, COL), P(COL, None), P(COL, ROW), P(ROW, COL)),
        check_vma=False,
    )
```

```python
import jax
import jax.numpy as jnp
from jax import lax
from jax.experimental import pallas as pl
from jax.experimental.pallas import tpu as pltpu
from jax.sharding import Mesh
from jax.sharding import PartitionSpec as P

DIN = 16384
COL = ("col_0", "col_1", "col_2")
ROW = ("row_0", "row_1")
ALL = ROW + COL
CORE = "col_2"
CHIPS = ("col_0", "col_1")

decay_part = 0.05
step_size = 0.01
epsilon = 1e-06

HIGH = lax.Precision.HIGH
HIGHEST = lax.Precision.HIGHEST


def whole(v):
    return jnp.broadcast_to(v, (8, 128))


def eliminate(z_ref, u_ref):
    lane = lax.broadcasted_iota(jnp.int32, (8, 128), 1)
    sub = lax.broadcasted_iota(jnp.int32, (8, 128), 0)
    rows = [[z_ref[t, 8 * q:8 * q + 8, :] for t in range(4)] for q in range(16)]
    for p in range(16):
        columns = {}
        for q in range(p, 16):
            for i in range(8):
                columns[q, i] = whole(rows[q][0][:, 8 * p + i:8 * p + i + 1])
        pivot = {(i, j): whole(columns[p, j][i:i + 1, :]) for j in range(8) for i in range(j, 8)}
        own = (lane >= 8 * p) & (lane < 8 * p + 8)
        start = [jnp.where(own, jnp.where(sub == lane - 8 * p, 1.0, 0.0), rows[p][0])] + rows[p][1:]
        inv = {}
        low = {}
        for j in range(8):
            r = lax.rsqrt(pivot[j, j])
            col = {i: pivot[i, j] * r for i in range(j + 1, 8)}
            for k in range(j + 1, 8):
                for i in range(k, 8):
                    pivot[i, k] = pivot[i, k] - col[i] * col[k]
            for m in range(j):
                inv[j, m] = pivot[j, m, "sum"] * (-r)
            inv[j, j] = r
            for i in range(j + 1, 8):
                for m in range(j + 1):
                    term = col[i] * inv[j, m]
                    pivot[i, m, "sum"] = term if m == j else pivot[i, m, "sum"] + term
        first = [[whole(start[t][i:i + 1, :]) for i in range(8)] for t in range(4)]
        solved = []
        for t in range(4):
            lows = []
            for i in range(8):
                v = inv[i, 0] * first[t][0]
                for m in range(1, i + 1):
                    v = v + inv[i, m] * first[t][m]
                lows.append(v)
            out = lows[0]
            for i in range(1, 8):
                out = jnp.where(sub == i, lows[i], out)
            u_ref[t, 8 * p:8 * p + 8, :] = jnp.where(lane <= sub + 8 * p, out, 0.0) if t == 0 else out
            line = []
            for i in range(8):
                v = inv[7, i] * lows[7]
                for m in range(i, 7):
                    v = v + inv[m, i] * lows[m]
                line.append(v)
            solved.append(line)
        for q in range(p + 1, 16):
            for t in range(4):
                total = jnp.where(own, 0.0, rows[q][t]) if t == 0 else rows[q][t]
                for i in range(8):
                    total = total - columns[q, i] * solved[t][i]
                rows[q][t] = total

def factor_kernel(g_ref, x_ref, z_ref, d_ref, u_ref):
    z_ref[...] = g_ref[...]
    def step(k, carry):
        at = pl.multiple_of(k * 128, 128)
        places = [pl.multiple_of(lax.rem(k + t, 4) * 128, 128) for t in range(4)]
        for t in range(4):
            d_ref[t] = z_ref[pl.ds(at, 128), pl.ds(places[t], 128)]
        eliminate(d_ref, u_ref)
        for t in range(4):
            x_ref[pl.ds(at, 128), pl.ds(places[t], 128)] = jnp.where(places[t] <= at, u_ref[t], 0.0)
        for t in range(1, 4):
            @pl.when(places[t] > at)
            def _():
                lower = u_ref[t]
                rest = pl.ds(places[t], 128)
                for s in range(4):
                    change = lax.dot_general(lower, u_ref[s], (((0,), (0,)), ((), ())), precision=HIGHEST, preferred_element_type=jnp.float32)
                    if s == 0:
                        z_ref[rest, pl.ds(places[s], 128)] = -change
                    else:
                        z_ref[rest, pl.ds(places[s], 128)] -= change
        return carry
    lax.fori_loop(0, 4, step, 0)


def inverse_factor(gram):
    return pl.pallas_call(
        factor_kernel,
        out_shape=jax.ShapeDtypeStruct((512, 512), jnp.float32),
        scratch_shapes=[
            pltpu.VMEM((512, 512), jnp.float32),
            pltpu.VMEM((4, 128, 128), jnp.float32),
            pltpu.VMEM((4, 128, 128), jnp.float32),
        ],
        compiler_params=pltpu.CompilerParams(vmem_limit_bytes=16 * 1024 * 1024),
    )(gram)


def dot(lhs, rhs, dims, precision=None):
    return lax.dot_general(
        lhs, rhs, ((dims[:1], dims[1:]), ((), ())), precision=precision, preferred_element_type=jnp.float32
    )


def scatter_sum(array, axes, length):
    pieces = array.reshape(length, array.shape[0] // length, *array.shape[1:])
    return jnp.sum(lax.all_to_all(pieces, axes, 0, 0, tiled=True).astype(jnp.float32), axis=0)


def gathered(array, axes, length):
    pieces = lax.all_to_all(
        jnp.broadcast_to(array[None], (length, *array.shape)), axes, 0, 0, tiled=True
    )
    return pieces.reshape(length * array.shape[0], *array.shape[1:])


def to_other_core(array):
    return lax.ppermute(array, CORE, [(0, 1), (1, 0)])


def in_core_order(own, other, core):
    return jnp.where(
        core == 0, jnp.concatenate([own, other], axis=0), jnp.concatenate([other, own], axis=0)
    )


def to_tile_owner(array):
    pairs = [(r * 16 + 2 * j + k, j * 16 + 2 * r + k) for r in range(8) for j in range(8) for k in range(2)]
    return lax.ppermute(array, ALL, pairs)


def in_two_parts(row):
    first = row.astype(jnp.bfloat16)
    second = (row - first.astype(jnp.float32)).astype(jnp.bfloat16)
    index = lax.broadcasted_iota(jnp.int32, (16, row.shape[0]), 0)
    zero = jnp.zeros((), jnp.bfloat16)
    return jnp.where(index == 0, first[None], jnp.where(index == 1, second[None], zero))


def split(array):
    first = array.astype(jnp.bfloat16)
    return first, (array - first.astype(jnp.float32)).astype(jnp.bfloat16)


def project_kernel(core_ref, first_ref, second_ref, own_ref, other_ref, out_ref):
    step = pl.program_id(0)
    left = jnp.where(step < 4, own_ref[...], other_ref[...])
    high = left.astype(jnp.bfloat16)
    low = (left - high.astype(jnp.float32)).astype(jnp.bfloat16)
    first = first_ref[...]
    part = jnp.dot(first, high, preferred_element_type=jnp.float32)
    part += jnp.dot(first, low, preferred_element_type=jnp.float32)
    part += jnp.dot(second_ref[...], high, preferred_element_type=jnp.float32)

    @pl.when(step == 0)
    def _():
        out_ref[...] = part

    @pl.when(step > 0)
    def _():
        out_ref[...] += part


def transposed_product(core, splits, own, other):
    def column(step, core_ref):
        half = lax.rem(core_ref[0] + step // 4, 2)
        return 0, half * 4 + lax.rem(step, 4)

    spec = pl.BlockSpec((1024, 256), column)
    return pl.pallas_call(
        project_kernel,
        out_shape=jax.ShapeDtypeStruct((1024, 512), jnp.float32),
        grid_spec=pltpu.PrefetchScalarGridSpec(
            num_scalar_prefetch=1,
            grid=(8,),
            in_specs=[
                spec,
                spec,
                pl.BlockSpec((256, 512), lambda step, core_ref: (jnp.minimum(step, 3), 0)),
                pl.BlockSpec((256, 512), lambda step, core_ref: (jnp.maximum(step - 4, 0), 0)),
            ],
            out_specs=pl.BlockSpec((1024, 512), lambda step, core_ref: (0, 0)),
        ),
        compiler_params=pltpu.CompilerParams(
            dimension_semantics=("arbitrary",), vmem_limit_bytes=24 * 1024 * 1024
        ),
    )(core[None], *splits, own, other)


def per_device(momentum, gradient, right_prev, weight, tokens):
    core = lax.axis_index(CORE)
    chip = lax.axis_index(CHIPS)

    def half(array, which):
        return lax.dynamic_slice_in_dim(array, which * 1024, 1024, 0)

    mixed = momentum.astype(jnp.float32) + gradient.astype(jnp.float32)
    partial_left = dot(mixed, right_prev, (1, 0), HIGH)
    partial_left = half(partial_left, core) + to_other_core(half(partial_left, 1 - core))
    partial_left, momentum, gradient = lax.optimization_barrier((partial_left, momentum, gradient))
    left_shard = scatter_sum(partial_left, CHIPS, 8)
    mixed_splits = split((momentum.astype(jnp.float32) + gradient.astype(jnp.float32)).T)
    left_shard, mixed_splits = lax.optimization_barrier((left_shard, mixed_splits))

    left_own = gathered(left_shard, CHIPS, 8)
    left_other = to_other_core(left_own)
    tile_left_raw = to_tile_owner(left_shard)

    gram_rows = core * 256 + chip * 32
    gram_block = sum(
        dot(lax.dynamic_slice_in_dim(part, gram_rows, 32, 1), part, (0, 0), HIGHEST)
        for part in (left_own, left_other)
    )
    gram_block, left_own, left_other = lax.optimization_barrier((gram_block, left_own, left_other))
    gram_block = jnp.sum(gathered(gram_block, ROW, 8).reshape(8, 32, 512), axis=0)
    gram_half = gathered(gram_block, CHIPS, 8)
    inverse = inverse_factor(in_core_order(gram_half, to_other_core(gram_half), core))

    partial_right = transposed_product(core, mixed_splits, left_own, left_other)
    right_shard = scatter_sum(partial_right, ROW, 8)

    right_own = dot(right_shard, inverse, (1, 1), HIGHEST)
    right_send = right_own.astype(jnp.bfloat16)
    left_send = dot(tile_left_raw, inverse, (1, 1), HIGH).astype(jnp.bfloat16)
    squares = in_two_parts(jnp.sum(right_own * right_own, axis=0))
    rows = gathered(jnp.concatenate([right_send, left_send, squares]), ROW, 8).reshape(8, 272, 512)
    right_factor = rows[:, :128].reshape(1024, 512)
    tile_left = rows[:, 128:256].reshape(1024, 512)
    squares = in_two_parts(jnp.sum(rows[:, 256:].astype(jnp.float32), axis=(0, 1)))

    tile = gathered(jnp.concatenate([to_tile_owner(right_send), squares]), CHIPS, 8).reshape(8, 144, 512)
    left_factor = [dot(part, inverse, (1, 1), HIGH).astype(jnp.bfloat16) for part in (left_own, left_other)]
    outer = dot(in_core_order(*left_factor, core), right_factor, (1, 1))
    mixed = momentum.astype(jnp.float32) + gradient.astype(jnp.float32)
    new_momentum = (mixed - decay_part * outer).astype(jnp.bfloat16)
    tile, new_momentum = lax.optimization_barrier((tile, new_momentum))

    own_squares = jnp.sum(tile[:, 128:].astype(jnp.float32), axis=(0, 1))
    own = tile[:, :128].reshape(1024, 512)
    other = to_other_core(jnp.concatenate([own, in_two_parts(own_squares)]))
    scale = lax.rsqrt(
        (own_squares + jnp.sum(other[1024:].astype(jnp.float32), axis=0)) / DIN + epsilon
    )
    tile_left = (tile_left.astype(jnp.float32) * scale).astype(jnp.bfloat16)
    update = dot(tile_left, in_core_order(own, other[:1024], core), (1, 1))
    new_weight = (weight.astype(jnp.float32) - step_size * update).astype(jnp.bfloat16)
    partial_projected = dot(tokens, new_weight, (1, 1)).astype(jnp.bfloat16)
    partial_projected, scale, right_factor = lax.optimization_barrier(
        (partial_projected, scale, right_factor)
    )
    projected = scatter_sum(partial_projected, ROW, 8).astype(jnp.bfloat16)
    new_basis = right_factor.astype(jnp.float32) * scale
    return (new_momentum, new_basis, new_weight, projected)


def solution(mesh):
    torus = Mesh(mesh.devices.reshape(4, 2, 4, 2, 2), ("row_0", "row_1", "col_0", "col_1", "col_2"))
    placed = (P(ROW, COL), P(ROW, COL), P(COL, None), P(COL, ROW), P(None, ROW))
    return jax.shard_map(
        per_device,
        mesh=torus,
        in_specs=placed,
        out_specs=(P(ROW, COL), P(COL, None), P(COL, ROW), P(ROW, COL)),
        check_vma=False,
    )
```

```python
import jax
import jax.numpy as jnp
from jax import lax
from jax.experimental import pallas as pl
from jax.experimental.pallas import tpu as pltpu
from jax.sharding import Mesh
from jax.sharding import PartitionSpec as P

DIN = 16384
COL = ("col_0", "col_1", "col_2")
ROW = ("row_0", "row_1")
ALL = ROW + COL
CORE = "col_2"
CHIPS = ("col_0", "col_1")

decay_part = 0.05
step_size = 0.01
epsilon = 1e-06

HIGH = lax.Precision.HIGH
HIGHEST = lax.Precision.HIGHEST


def whole(v):
    return jnp.broadcast_to(v, (8, 128))


def eliminate(z_ref, u_ref):
    lane = lax.broadcasted_iota(jnp.int32, (8, 128), 1)
    sub = lax.broadcasted_iota(jnp.int32, (8, 128), 0)
    rows = [[z_ref[t, 8 * q:8 * q + 8, :] for t in range(4)] for q in range(16)]
    for p in range(16):
        columns = {}
        for q in range(p, 16):
            for i in range(8):
                columns[q, i] = whole(rows[q][0][:, 8 * p + i:8 * p + i + 1])
        pivot = {(i, j): whole(columns[p, j][i:i + 1, :]) for j in range(8) for i in range(j, 8)}
        own = (lane >= 8 * p) & (lane < 8 * p + 8)
        start = [jnp.where(own, jnp.where(sub == lane - 8 * p, 1.0, 0.0), rows[p][0])] + rows[p][1:]
        inv = {}
        low = {}
        for j in range(8):
            r = lax.rsqrt(pivot[j, j])
            col = {i: pivot[i, j] * r for i in range(j + 1, 8)}
            for k in range(j + 1, 8):
                for i in range(k, 8):
                    pivot[i, k] = pivot[i, k] - col[i] * col[k]
            for m in range(j):
                inv[j, m] = pivot[j, m, "sum"] * (-r)
            inv[j, j] = r
            for i in range(j + 1, 8):
                for m in range(j + 1):
                    term = col[i] * inv[j, m]
                    pivot[i, m, "sum"] = term if m == j else pivot[i, m, "sum"] + term
        first = [[whole(start[t][i:i + 1, :]) for i in range(8)] for t in range(4)]
        solved = []
        for t in range(4):
            lows = []
            for i in range(8):
                v = inv[i, 0] * first[t][0]
                for m in range(1, i + 1):
                    v = v + inv[i, m] * first[t][m]
                lows.append(v)
            out = lows[0]
            for i in range(1, 8):
                out = jnp.where(sub == i, lows[i], out)
            u_ref[t, 8 * p:8 * p + 8, :] = jnp.where(lane <= sub + 8 * p, out, 0.0) if t == 0 else out
            line = []
            for i in range(8):
                v = inv[7, i] * lows[7]
                for m in range(i, 7):
                    v = v + inv[m, i] * lows[m]
                line.append(v)
            solved.append(line)
        for q in range(p + 1, 16):
            for t in range(4):
                total = jnp.where(own, 0.0, rows[q][t]) if t == 0 else rows[q][t]
                for i in range(8):
                    total = total - columns[q, i] * solved[t][i]
                rows[q][t] = total

def factor_kernel(g_ref, x_ref, z_ref, d_ref, u_ref):
    z_ref[...] = g_ref[...]
    def step(k, carry):
        at = pl.multiple_of(k * 128, 128)
        places = [pl.multiple_of(lax.rem(k + t, 4) * 128, 128) for t in range(4)]
        for t in range(4):
            d_ref[t] = z_ref[pl.ds(at, 128), pl.ds(places[t], 128)]
        eliminate(d_ref, u_ref)
        for t in range(4):
            x_ref[pl.ds(at, 128), pl.ds(places[t], 128)] = jnp.where(places[t] <= at, u_ref[t], 0.0)
        for t in range(1, 4):
            @pl.when(places[t] > at)
            def _():
                lower = u_ref[t]
                rest = pl.ds(places[t], 128)
                for s in range(4):
                    change = lax.dot_general(lower, u_ref[s], (((0,), (0,)), ((), ())), precision=HIGHEST, preferred_element_type=jnp.float32)
                    if s == 0:
                        z_ref[rest, pl.ds(places[s], 128)] = -change
                    else:
                        z_ref[rest, pl.ds(places[s], 128)] -= change
        return carry
    lax.fori_loop(0, 4, step, 0)


def inverse_factor(gram):
    return pl.pallas_call(
        factor_kernel,
        out_shape=jax.ShapeDtypeStruct((512, 512), jnp.float32),
        scratch_shapes=[
            pltpu.VMEM((512, 512), jnp.float32),
            pltpu.VMEM((4, 128, 128), jnp.float32),
            pltpu.VMEM((4, 128, 128), jnp.float32),
        ],
        compiler_params=pltpu.CompilerParams(vmem_limit_bytes=16 * 1024 * 1024),
    )(gram)


def dot(lhs, rhs, dims, precision=None):
    return lax.dot_general(
        lhs, rhs, ((dims[:1], dims[1:]), ((), ())), precision=precision, preferred_element_type=jnp.float32
    )


def scatter_sum(array, axes, length):
    pieces = array.reshape(length, array.shape[0] // length, *array.shape[1:])
    return jnp.sum(lax.all_to_all(pieces, axes, 0, 0, tiled=True).astype(jnp.float32), axis=0)


def gathered(array, axes, length):
    pieces = lax.all_to_all(
        jnp.broadcast_to(array[None], (length, *array.shape)), axes, 0, 0, tiled=True
    )
    return pieces.reshape(length * array.shape[0], *array.shape[1:])


def to_other_core(array):
    return lax.ppermute(array, CORE, [(0, 1), (1, 0)])


def in_core_order(own, other, core):
    return jnp.where(
        core == 0, jnp.concatenate([own, other], axis=0), jnp.concatenate([other, own], axis=0)
    )


def to_tile_owner(array):
    pairs = [(r * 16 + 2 * j + k, j * 16 + 2 * r + k) for r in range(8) for j in range(8) for k in range(2)]
    return lax.ppermute(array, ALL, pairs)


def in_two_parts(row):
    first = row.astype(jnp.bfloat16)
    second = (row - first.astype(jnp.float32)).astype(jnp.bfloat16)
    index = lax.broadcasted_iota(jnp.int32, (16, row.shape[0]), 0)
    zero = jnp.zeros((), jnp.bfloat16)
    return jnp.where(index == 0, first[None], jnp.where(index == 1, second[None], zero))


def split(array):
    first = array.astype(jnp.bfloat16)
    return first, (array - first.astype(jnp.float32)).astype(jnp.bfloat16)


def in_hbm(array):
    return pltpu.with_memory_space_constraint(array, pltpu.HBM)


def left_kernel(which_ref, momentum_ref, gradient_ref, right_ref, out_ref, high_ref, low_ref):
    @pl.when(pl.program_id(0) == 0)
    def _():
        right = right_ref[...]
        high = right.astype(jnp.bfloat16)
        high_ref[...] = high
        low_ref[...] = (right - high.astype(jnp.float32)).astype(jnp.bfloat16)

    mixed = momentum_ref[...].astype(jnp.float32) + gradient_ref[...].astype(jnp.float32)
    first = mixed.astype(jnp.bfloat16)
    second = (mixed - first.astype(jnp.float32)).astype(jnp.bfloat16)
    part = jnp.dot(first, high_ref[...], preferred_element_type=jnp.float32)
    part += jnp.dot(first, low_ref[...], preferred_element_type=jnp.float32)
    part += jnp.dot(second, high_ref[...], preferred_element_type=jnp.float32)
    out_ref[...] = part


def half_product(which, momentum, gradient, right):
    rows = pl.BlockSpec((256, 1024), lambda step, which_ref: (which_ref[0] * 4 + step, 0))
    return pl.pallas_call(
        left_kernel,
        out_shape=jax.ShapeDtypeStruct((1024, 512), jnp.float32),
        grid_spec=pltpu.PrefetchScalarGridSpec(
            num_scalar_prefetch=1,
            grid=(4,),
            in_specs=[rows, rows, pl.BlockSpec((1024, 512), lambda step, which_ref: (0, 0))],
            out_specs=pl.BlockSpec((256, 512), lambda step, which_ref: (step, 0)),
            scratch_shapes=[pltpu.VMEM((1024, 512), jnp.bfloat16)] * 2,
        ),
        compiler_params=pltpu.CompilerParams(
            dimension_semantics=("arbitrary",), vmem_limit_bytes=24 * 1024 * 1024
        ),
    )(which[None], *(in_hbm(array) for array in (momentum, gradient, right)))


def project_kernel(core_ref, first_ref, second_ref, own_ref, other_ref, out_ref):
    step = pl.program_id(0)
    left = jnp.where(step < 2, own_ref[...], other_ref[...])
    high = left.astype(jnp.bfloat16)
    low = (left - high.astype(jnp.float32)).astype(jnp.bfloat16)
    first = first_ref[...]
    part = jnp.dot(first, high, preferred_element_type=jnp.float32)
    part += jnp.dot(first, low, preferred_element_type=jnp.float32)
    part += jnp.dot(second_ref[...], high, preferred_element_type=jnp.float32)

    @pl.when(step == 0)
    def _():
        out_ref[...] = part

    @pl.when(step > 0)
    def _():
        out_ref[...] += part


def transposed_product(core, splits, own, other):
    def column(step, core_ref):
        half = lax.rem(core_ref[0] + step // 2, 2)
        return 0, half * 2 + lax.rem(step, 2)

    spec = pl.BlockSpec((1024, 512), column)
    return pl.pallas_call(
        project_kernel,
        out_shape=jax.ShapeDtypeStruct((1024, 512), jnp.float32),
        grid_spec=pltpu.PrefetchScalarGridSpec(
            num_scalar_prefetch=1,
            grid=(4,),
            in_specs=[
                spec,
                spec,
                pl.BlockSpec((512, 512), lambda step, core_ref: (jnp.minimum(step, 1), 0)),
                pl.BlockSpec((512, 512), lambda step, core_ref: (jnp.maximum(step - 2, 0), 0)),
            ],
            out_specs=pl.BlockSpec((1024, 512), lambda step, core_ref: (0, 0)),
        ),
        compiler_params=pltpu.CompilerParams(
            dimension_semantics=("arbitrary",), vmem_limit_bytes=32 * 1024 * 1024
        ),
    )(core[None], *(in_hbm(array) for array in splits), own, other)


def send_kernel(pieces_ref, left_ref, inverse_ref, right_ref, out_ref, held_ref):
    @pl.when(pl.program_id(0) == 0)
    def _():
        contract = (((1,), (1,)), ((), ()))
        total = pieces_ref[0]
        for i in range(1, 8):
            total = total + pieces_ref[i]
        right = lax.dot_general(
            total, inverse_ref[...], contract, precision=HIGHEST, preferred_element_type=jnp.float32
        )
        left = lax.dot_general(
            left_ref[...], inverse_ref[...], contract, precision=HIGHEST, preferred_element_type=jnp.float32
        )
        squares = jnp.sum(right * right, axis=0, keepdims=True)
        first = squares.astype(jnp.bfloat16).astype(jnp.float32)
        index = lax.broadcasted_iota(jnp.int32, (16, 512), 0)
        parts = jnp.where(index == 0, first, jnp.where(index == 1, squares - first, 0.0))
        right_ref[...] = right.astype(jnp.bfloat16)
        held_ref[0:128, :] = right.astype(jnp.bfloat16)
        held_ref[128:256, :] = left.astype(jnp.bfloat16)
        held_ref[256:272, :] = parts.astype(jnp.bfloat16)

    out_ref[0] = held_ref[...]


def right_and_left_to_send(pieces, left, inverse):
    return pl.pallas_call(
        send_kernel,
        out_shape=(
            jax.ShapeDtypeStruct((128, 512), jnp.bfloat16),
            jax.ShapeDtypeStruct((8, 272, 512), jnp.bfloat16),
        ),
        grid=(8,),
        in_specs=[
            pl.BlockSpec((8, 128, 512), lambda copy: (0, 0, 0)),
            pl.BlockSpec((128, 512), lambda copy: (0, 0)),
            pl.BlockSpec((512, 512), lambda copy: (0, 0)),
        ],
        out_specs=(
            pl.BlockSpec((128, 512), lambda copy: (0, 0)),
            pl.BlockSpec((1, 272, 512), lambda copy: (copy, 0, 0)),
        ),
        scratch_shapes=[pltpu.VMEM((272, 512), jnp.bfloat16)],
        compiler_params=pltpu.CompilerParams(
            dimension_semantics=("arbitrary",), vmem_limit_bytes=24 * 1024 * 1024
        ),
    )(pieces, left, inverse)


def per_device(momentum, gradient, right_prev, weight, tokens):
    core = lax.axis_index(CORE)
    chip = lax.axis_index(CHIPS)

    partial_other = to_other_core(half_product(1 - core, momentum, gradient, right_prev))
    partial_left = half_product(core, momentum, gradient, right_prev) + partial_other
    partial_left, late_momentum, late_gradient = lax.optimization_barrier((partial_left, momentum, gradient))
    left_shard = scatter_sum(partial_left, CHIPS, 8)
    mixed_splits = split((late_momentum.astype(jnp.float32) + late_gradient.astype(jnp.float32)).T)
    left_shard, mixed_splits = lax.optimization_barrier((left_shard, mixed_splits))

    left_own = gathered(left_shard, CHIPS, 8)
    left_other = to_other_core(left_own)
    tile_left_raw = to_tile_owner(left_shard)

    gram_rows = core * 256 + chip * 32
    gram_block = sum(
        dot(lax.dynamic_slice_in_dim(part, gram_rows, 32, 1), part, (0, 0), HIGHEST)
        for part in (left_own, left_other)
    )
    gram_block, left_own, left_other = lax.optimization_barrier((gram_block, left_own, left_other))
    gram_block = jnp.sum(gathered(gram_block, ROW, 8).reshape(8, 32, 512), axis=0)
    partial_right = transposed_product(core, mixed_splits, left_own, left_other)
    gram_block, partial_right = lax.optimization_barrier((gram_block, partial_right))
    gram_half = gathered(gram_block, CHIPS, 8)
    inverse = inverse_factor(in_core_order(gram_half, to_other_core(gram_half), core))

    pieces = lax.all_to_all(partial_right.reshape(8, 128, 512), ROW, 0, 0, tiled=True)
    right_send, copies = right_and_left_to_send(pieces, tile_left_raw, inverse)
    rows = lax.all_to_all(copies, ROW, 0, 0, tiled=True)
    tile_right = to_tile_owner(right_send)
    left_factor = [dot(part, inverse, (1, 1), HIGH).astype(jnp.bfloat16) for part in (left_own, left_other)]
    left_factor = in_core_order(*left_factor, core)
    rows, tile_right = lax.optimization_barrier((rows, tile_right))
    right_factor = rows[:, :128].reshape(1024, 512)
    tile_left = rows[:, 128:256].reshape(1024, 512)
    squares = in_two_parts(jnp.sum(rows[:, 256:].astype(jnp.float32), axis=(0, 1)))

    tile = gathered(jnp.concatenate([tile_right, squares]), CHIPS, 8).reshape(8, 144, 512)
    outer = dot(left_factor, right_factor, (1, 1))
    mixed = momentum.astype(jnp.float32) + gradient.astype(jnp.float32)
    new_momentum = (mixed - decay_part * outer).astype(jnp.bfloat16)
    tile, new_momentum = lax.optimization_barrier((tile, new_momentum))

    own_squares = jnp.sum(tile[:, 128:].astype(jnp.float32), axis=(0, 1))
    own = tile[:, :128].reshape(1024, 512)
    other = to_other_core(jnp.concatenate([own, in_two_parts(own_squares)]))
    scale = lax.rsqrt(
        (own_squares + jnp.sum(other[1024:].astype(jnp.float32), axis=0)) / DIN + epsilon
    )
    tile_left = (tile_left.astype(jnp.float32) * scale).astype(jnp.bfloat16)
    update = dot(tile_left, in_core_order(own, other[:1024], core), (1, 1))
    new_weight = (weight.astype(jnp.float32) - step_size * update).astype(jnp.bfloat16)
    partial_projected = dot(tokens, new_weight, (1, 1)).astype(jnp.bfloat16)
    projected = scatter_sum(partial_projected, ROW, 8).astype(jnp.bfloat16)
    new_basis = right_factor.astype(jnp.float32) * scale
    return (new_momentum, new_basis, new_weight, projected)


def solution(mesh):
    torus = Mesh(mesh.devices.reshape(4, 2, 4, 2, 2), ("row_0", "row_1", "col_0", "col_1", "col_2"))
    placed = (P(ROW, COL), P(ROW, COL), P(COL, None), P(COL, ROW), P(None, ROW))
    return jax.shard_map(
        per_device,
        mesh=torus,
        in_specs=placed,
        out_specs=(P(ROW, COL), P(COL, None), P(COL, ROW), P(ROW, COL)),
        check_vma=False,
    )
```

```python
import jax
import jax.numpy as jnp
from jax import lax
from jax.experimental import pallas as pl
from jax.experimental.pallas import tpu as pltpu
from jax.sharding import Mesh
from jax.sharding import PartitionSpec as P

DIN = 16384
COL = ("col_0", "col_1", "col_2")
ROW = ("row_0", "row_1")
ALL = ROW + COL
CORE = "col_2"
CHIPS = ("col_0", "col_1")

decay_part = 0.05
step_size = 0.01
epsilon = 1e-06

HIGH = lax.Precision.HIGH
HIGHEST = lax.Precision.HIGHEST


def whole(v):
    return jnp.broadcast_to(v, (8, 128))


def eliminate(z_ref, u_ref):
    lane = lax.broadcasted_iota(jnp.int32, (8, 128), 1)
    sub = lax.broadcasted_iota(jnp.int32, (8, 128), 0)
    rows = [[z_ref[t, 8 * q:8 * q + 8, :] for t in range(4)] for q in range(16)]
    for p in range(16):
        columns = {}
        for q in range(p, 16):
            for i in range(8):
                columns[q, i] = whole(rows[q][0][:, 8 * p + i:8 * p + i + 1])
        pivot = {(i, j): whole(columns[p, j][i:i + 1, :]) for j in range(8) for i in range(j, 8)}
        own = (lane >= 8 * p) & (lane < 8 * p + 8)
        start = [jnp.where(own, jnp.where(sub == lane - 8 * p, 1.0, 0.0), rows[p][0])] + rows[p][1:]
        inv = {}
        low = {}
        for j in range(8):
            r = lax.rsqrt(pivot[j, j])
            col = {i: pivot[i, j] * r for i in range(j + 1, 8)}
            for k in range(j + 1, 8):
                for i in range(k, 8):
                    pivot[i, k] = pivot[i, k] - col[i] * col[k]
            for m in range(j):
                inv[j, m] = pivot[j, m, "sum"] * (-r)
            inv[j, j] = r
            for i in range(j + 1, 8):
                for m in range(j + 1):
                    term = col[i] * inv[j, m]
                    pivot[i, m, "sum"] = term if m == j else pivot[i, m, "sum"] + term
        first = [[whole(start[t][i:i + 1, :]) for i in range(8)] for t in range(4)]
        solved = []
        for t in range(4):
            lows = []
            for i in range(8):
                v = inv[i, 0] * first[t][0]
                for m in range(1, i + 1):
                    v = v + inv[i, m] * first[t][m]
                lows.append(v)
            out = lows[0]
            for i in range(1, 8):
                out = jnp.where(sub == i, lows[i], out)
            u_ref[t, 8 * p:8 * p + 8, :] = jnp.where(lane <= sub + 8 * p, out, 0.0) if t == 0 else out
            line = []
            for i in range(8):
                v = inv[7, i] * lows[7]
                for m in range(i, 7):
                    v = v + inv[m, i] * lows[m]
                line.append(v)
            solved.append(line)
        for q in range(p + 1, 16):
            for t in range(4):
                total = jnp.where(own, 0.0, rows[q][t]) if t == 0 else rows[q][t]
                for i in range(8):
                    total = total - columns[q, i] * solved[t][i]
                rows[q][t] = total

def factor_kernel(core_ref, own_ref, other_ref, x_ref, z_ref, d_ref, u_ref):
    start = pl.multiple_of(core_ref[0] * 256, 256)
    z_ref[pl.ds(start, 256), :] = own_ref[...]
    z_ref[pl.ds(pl.multiple_of(256 - start, 256), 256), :] = other_ref[...]
    def step(k, carry):
        at = pl.multiple_of(k * 128, 128)
        places = [pl.multiple_of(lax.rem(k + t, 4) * 128, 128) for t in range(4)]
        for t in range(4):
            d_ref[t] = z_ref[pl.ds(at, 128), pl.ds(places[t], 128)]
        eliminate(d_ref, u_ref)
        for t in range(4):
            x_ref[pl.ds(at, 128), pl.ds(places[t], 128)] = jnp.where(places[t] <= at, u_ref[t], 0.0)
        for t in range(1, 4):
            @pl.when(places[t] > at)
            def _():
                lower = u_ref[t]
                rest = pl.ds(places[t], 128)
                for s in range(4):
                    change = lax.dot_general(lower, u_ref[s], (((0,), (0,)), ((), ())), precision=HIGHEST, preferred_element_type=jnp.float32)
                    if s == 0:
                        z_ref[rest, pl.ds(places[s], 128)] = -change
                    else:
                        z_ref[rest, pl.ds(places[s], 128)] -= change
        return carry
    lax.fori_loop(0, 4, step, 0)


def inverse_factor(core, own, other):
    half = pl.BlockSpec((256, 512), lambda step, core_ref: (0, 0))
    return pl.pallas_call(
        factor_kernel,
        out_shape=jax.ShapeDtypeStruct((512, 512), jnp.float32),
        grid_spec=pltpu.PrefetchScalarGridSpec(
            num_scalar_prefetch=1,
            grid=(1,),
            in_specs=[half, half],
            out_specs=pl.BlockSpec((512, 512), lambda step, core_ref: (0, 0)),
            scratch_shapes=[
                pltpu.VMEM((512, 512), jnp.float32),
                pltpu.VMEM((4, 128, 128), jnp.float32),
                pltpu.VMEM((4, 128, 128), jnp.float32),
            ],
        ),
        compiler_params=pltpu.CompilerParams(vmem_limit_bytes=16 * 1024 * 1024),
    )(core[None], own, other)


def dot(lhs, rhs, dims, precision=None):
    return lax.dot_general(
        lhs, rhs, ((dims[:1], dims[1:]), ((), ())), precision=precision, preferred_element_type=jnp.float32
    )


def scatter_sum(array, axes, length):
    pieces = array.reshape(length, array.shape[0] // length, *array.shape[1:])
    return jnp.sum(lax.all_to_all(pieces, axes, 0, 0, tiled=True).astype(jnp.float32), axis=0)


def gathered(array, axes, length):
    pieces = lax.all_to_all(
        jnp.broadcast_to(array[None], (length, *array.shape)), axes, 0, 0, tiled=True
    )
    return pieces.reshape(length * array.shape[0], *array.shape[1:])


def to_other_core(array):
    return lax.ppermute(array, CORE, [(0, 1), (1, 0)])


def in_core_order(own, other, core):
    return jnp.where(
        core == 0, jnp.concatenate([own, other], axis=0), jnp.concatenate([other, own], axis=0)
    )


def to_tile_owner(array):
    pairs = [(r * 16 + 2 * j + k, j * 16 + 2 * r + k) for r in range(8) for j in range(8) for k in range(2)]
    return lax.ppermute(array, ALL, pairs)


def in_two_parts(row):
    first = row.astype(jnp.bfloat16)
    second = (row - first.astype(jnp.float32)).astype(jnp.bfloat16)
    index = lax.broadcasted_iota(jnp.int32, (16, row.shape[0]), 0)
    zero = jnp.zeros((), jnp.bfloat16)
    return jnp.where(index == 0, first[None], jnp.where(index == 1, second[None], zero))


def in_hbm(array):
    return pltpu.with_memory_space_constraint(array, pltpu.HBM)


def left_kernel(which_ref, momentum_ref, gradient_ref, right_ref, out_ref, parts_ref):
    @pl.when(pl.program_id(0) == 0)
    def _():
        right = right_ref[...]
        high = right.astype(jnp.bfloat16)
        parts_ref[0:1024, :] = high
        parts_ref[1024:2048, :] = (right - high.astype(jnp.float32)).astype(jnp.bfloat16)
        parts_ref[2048:3072, :] = high

    mixed = momentum_ref[...].astype(jnp.float32) + gradient_ref[...].astype(jnp.float32)
    first = mixed.astype(jnp.bfloat16)
    second = (mixed - first.astype(jnp.float32)).astype(jnp.bfloat16)
    out_ref[...] = jnp.dot(
        jnp.concatenate([first, first, second], axis=1), parts_ref[...], preferred_element_type=jnp.float32
    )


def half_product(which, momentum, gradient, right):
    rows = pl.BlockSpec((256, 1024), lambda step, which_ref: (which_ref[0] * 4 + step, 0))
    return pl.pallas_call(
        left_kernel,
        out_shape=jax.ShapeDtypeStruct((1024, 512), jnp.float32),
        grid_spec=pltpu.PrefetchScalarGridSpec(
            num_scalar_prefetch=1,
            grid=(4,),
            in_specs=[rows, rows, pl.BlockSpec((1024, 512), lambda step, which_ref: (0, 0))],
            out_specs=pl.BlockSpec((256, 512), lambda step, which_ref: (step, 0)),
            scratch_shapes=[pltpu.VMEM((3072, 512), jnp.bfloat16)],
        ),
        compiler_params=pltpu.CompilerParams(
            dimension_semantics=("arbitrary",), vmem_limit_bytes=24 * 1024 * 1024
        ),
    )(which[None], *(in_hbm(array) for array in (momentum, gradient, right)))


def project_kernel(core_ref, momentum_ref, gradient_ref, own_ref, other_ref, out_ref):
    step = pl.program_id(0)
    left = jnp.where(step < 4, own_ref[...], other_ref[...])
    high = left.astype(jnp.bfloat16)
    low = (left - high.astype(jnp.float32)).astype(jnp.bfloat16)
    mixed = momentum_ref[...].astype(jnp.float32) + gradient_ref[...].astype(jnp.float32)
    first = mixed.astype(jnp.bfloat16)
    second = (mixed - first.astype(jnp.float32)).astype(jnp.bfloat16)
    part = lax.dot_general(
        jnp.concatenate([first, first, second], axis=0),
        jnp.concatenate([high, low, high], axis=0),
        (((0,), (0,)), ((), ())),
        preferred_element_type=jnp.float32,
    )

    @pl.when(step == 0)
    def _():
        out_ref[...] = part

    @pl.when(step > 0)
    def _():
        out_ref[...] += part


def transposed_product(core, momentum, gradient, own, other):
    def rows(step, core_ref):
        half = lax.rem(core_ref[0] + step // 4, 2)
        return half * 4 + lax.rem(step, 4), 0

    spec = pl.BlockSpec((256, 1024), rows)
    return pl.pallas_call(
        project_kernel,
        out_shape=pltpu.HBM((1024, 512), jnp.float32),
        grid_spec=pltpu.PrefetchScalarGridSpec(
            num_scalar_prefetch=1,
            grid=(8,),
            in_specs=[
                spec,
                spec,
                pl.BlockSpec((256, 512), lambda step, core_ref: (jnp.minimum(step, 3), 0)),
                pl.BlockSpec((256, 512), lambda step, core_ref: (jnp.maximum(step - 4, 0), 0)),
            ],
            out_specs=pl.BlockSpec((1024, 512), lambda step, core_ref: (0, 0)),
        ),
        compiler_params=pltpu.CompilerParams(
            dimension_semantics=("arbitrary",), vmem_limit_bytes=32 * 1024 * 1024
        ),
    )(core[None], *(in_hbm(array) for array in (momentum, gradient)), own, other)


def send_kernel(pieces_ref, left_ref, inverse_ref, right_ref, out_ref, held_ref):
    @pl.when(pl.program_id(0) == 0)
    def _():
        contract = (((1,), (1,)), ((), ()))
        total = pieces_ref[0]
        for i in range(1, 8):
            total = total + pieces_ref[i]
        right = lax.dot_general(
            total, inverse_ref[...], contract, precision=HIGHEST, preferred_element_type=jnp.float32
        )
        left = lax.dot_general(
            left_ref[...], inverse_ref[...], contract, precision=HIGHEST, preferred_element_type=jnp.float32
        )
        squares = jnp.sum(right * right, axis=0, keepdims=True)
        first = squares.astype(jnp.bfloat16).astype(jnp.float32)
        index = lax.broadcasted_iota(jnp.int32, (16, 512), 0)
        parts = jnp.where(index == 0, first, jnp.where(index == 1, squares - first, 0.0))
        right_ref[...] = right.astype(jnp.bfloat16)
        held_ref[0:128, :] = right.astype(jnp.bfloat16)
        held_ref[128:256, :] = left.astype(jnp.bfloat16)
        held_ref[256:272, :] = parts.astype(jnp.bfloat16)

    out_ref[0] = held_ref[...]


def right_and_left_to_send(pieces, left, inverse):
    return pl.pallas_call(
        send_kernel,
        out_shape=(
            jax.ShapeDtypeStruct((128, 512), jnp.bfloat16),
            jax.ShapeDtypeStruct((8, 272, 512), jnp.bfloat16),
        ),
        grid=(8,),
        in_specs=[
            pl.BlockSpec((8, 128, 512), lambda copy: (0, 0, 0)),
            pl.BlockSpec((128, 512), lambda copy: (0, 0)),
            pl.BlockSpec((512, 512), lambda copy: (0, 0)),
        ],
        out_specs=(
            pl.BlockSpec((128, 512), lambda copy: (0, 0)),
            pl.BlockSpec((1, 272, 512), lambda copy: (copy, 0, 0)),
        ),
        scratch_shapes=[pltpu.VMEM((272, 512), jnp.bfloat16)],
        compiler_params=pltpu.CompilerParams(
            dimension_semantics=("arbitrary",), vmem_limit_bytes=24 * 1024 * 1024
        ),
    )(pieces, left, inverse)


def per_device(momentum, gradient, right_prev, weight, tokens):
    core = lax.axis_index(CORE)
    chip = lax.axis_index(CHIPS)

    partial_other = to_other_core(half_product(1 - core, momentum, gradient, right_prev))
    partial_left = half_product(core, momentum, gradient, right_prev) + partial_other
    left_shard = scatter_sum(partial_left, CHIPS, 8)
    left_own = gathered(left_shard, CHIPS, 8)
    left_other = to_other_core(left_own)
    tile_left_raw = to_tile_owner(left_shard)

    gram_rows = core * 256 + chip * 32
    gram_block = sum(
        dot(lax.dynamic_slice_in_dim(part, gram_rows, 32, 1), part, (0, 0), HIGH)
        for part in (left_own, left_other)
    )
    gram_block, left_own, left_other = lax.optimization_barrier((gram_block, left_own, left_other))
    gram_block = jnp.sum(gathered(gram_block, ROW, 8).reshape(8, 32, 512), axis=0)
    partial_right = transposed_product(core, momentum, gradient, left_own, left_other)
    gram_block, partial_right = lax.optimization_barrier((gram_block, partial_right))
    gram_half = gathered(gram_block, CHIPS, 8)
    inverse = inverse_factor(core, gram_half, to_other_core(gram_half))

    pieces = lax.all_to_all(partial_right.reshape(8, 128, 512), ROW, 0, 0, tiled=True)
    right_send, copies = right_and_left_to_send(pieces, tile_left_raw, inverse)
    rows = lax.all_to_all(copies, ROW, 0, 0, tiled=True)
    tile_right = to_tile_owner(right_send)
    left_factor = [dot(part, inverse, (1, 1), HIGH).astype(jnp.bfloat16) for part in (left_own, left_other)]
    left_factor = in_core_order(*left_factor, core)
    rows, tile_right = lax.optimization_barrier((rows, tile_right))
    right_factor = rows[:, :128].reshape(1024, 512)
    tile_left = rows[:, 128:256].reshape(1024, 512)
    squares = in_two_parts(jnp.sum(rows[:, 256:].astype(jnp.float32), axis=(0, 1)))

    tile = gathered(jnp.concatenate([tile_right, squares]), CHIPS, 8).reshape(8, 144, 512)
    outer = dot(left_factor, right_factor, (1, 1))
    mixed = momentum.astype(jnp.float32) + gradient.astype(jnp.float32)
    new_momentum = (mixed - decay_part * outer).astype(jnp.bfloat16)
    tile, new_momentum = lax.optimization_barrier((tile, new_momentum))

    own_squares = jnp.sum(tile[:, 128:].astype(jnp.float32), axis=(0, 1))
    own = tile[:, :128].reshape(1024, 512)
    other = to_other_core(jnp.concatenate([own, in_two_parts(own_squares)]))
    scale = lax.rsqrt(
        (own_squares + jnp.sum(other[1024:].astype(jnp.float32), axis=0)) / DIN + epsilon
    )
    tile_left = (tile_left.astype(jnp.float32) * scale).astype(jnp.bfloat16)
    update = dot(tile_left, in_core_order(own, other[:1024], core), (1, 1))
    new_weight = (weight.astype(jnp.float32) - step_size * update).astype(jnp.bfloat16)
    partial_projected = dot(tokens, new_weight, (1, 1)).astype(jnp.bfloat16)
    projected = scatter_sum(partial_projected, ROW, 8).astype(jnp.bfloat16)
    new_basis = right_factor.astype(jnp.float32) * scale
    return (new_momentum, new_basis, new_weight, projected)


def solution(mesh):
    torus = Mesh(mesh.devices.reshape(4, 2, 4, 2, 2), ("row_0", "row_1", "col_0", "col_1", "col_2"))
    placed = (P(ROW, COL), P(ROW, COL), P(COL, None), P(COL, ROW), P(None, ROW))
    return jax.shard_map(
        per_device,
        mesh=torus,
        in_specs=placed,
        out_specs=(P(ROW, COL), P(COL, None), P(COL, ROW), P(ROW, COL)),
        check_vma=False,
    )
```
